512 devices in a mesh: tm: 64 (over y, z), head: 8 (over x, core).
Axes of the slice: x: 4, y: 4, z: 16, core: 2. Of those that a mesh axis runs over, the one named last changes fastest.
Arguments:
- queries: bfloat16 [8192, 4096], P('tm', 'head'), may hold values from -6 to 6
- keys: bfloat16 [8192, 4096], P('tm', 'head'), may hold values from -6 to 6
- values: bfloat16 [8192, 4096], P('tm', 'head'), may hold values from -6 to 6
- log_decay: float32 [32, 8192], P('head', 'tm'), may hold values from -1 to 0
- agent_ids: int32 [8192], P('tm'), may hold values from 0 to 127
- norm_gain: float32 [4096], P('head'), may hold values from 0.1 to 1.9
- out_grad: bfloat16 [8192, 4096], P('tm', 'head'), may hold values from -6 to 6
Outputs:
- result: bfloat16 [8192, 4096], P('tm', 'head')
- query_grad: bfloat16 [8192, 4096], P('tm', 'head')
- key_grad: bfloat16 [8192, 4096], P('tm', 'head')
- value_grad: bfloat16 [8192, 4096], P('tm', 'head')
- decay_grad: float32 [32, 8192], P('head', 'tm')
- gain_grad: float32 [4096], P('head')
The draws below stay inside these ranges and needn't reach their ends.
All inputs are finite; a program needn't handle non-finite values.
Results may differ from the reference program's by a relative error of at most 0.001.
Values sent between devices are 32-bit elements; how exact they have to be, the bound alone decides.
No kernel may reach another device: no remote copies, remote signals or barrier semaphores. Data moves between devices by JAX's collectives and lax.ppermute only.
A program may use at most 128 MiB of HBM per device.

```python
import math
import jax
import jax.numpy as jnp
from jax import lax

ATTENTION_GROUPS = 32
DK = 128
GROUP = 128
AGENTS = 128
TEAM = 16
WIDTH = 4096
SEQUENCE_STEPS = 8192


def draw_log_decay(key, part):
    number_of_pieces = jax.random.split(key, 7)
    fast = jax.random.uniform(number_of_pieces[1], (ATTENTION_GROUPS, 1)) < 0.4
    slow_rate = jnp.exp(jax.random.uniform(number_of_pieces[0], (ATTENTION_GROUPS, 1), minval=math.log(1e-06), maxval=math.log(1e-05)))
    fast_rate = jnp.exp(jax.random.uniform(number_of_pieces[2], (ATTENTION_GROUPS, 1), minval=math.log(0.012), maxval=math.log(0.025)))
    starting_position = jnp.where(fast, fast_rate, slow_rate)
    approximate_guess = jax.random.uniform(number_of_pieces[3], (ATTENTION_GROUPS, SEQUENCE_STEPS), minval=0.3, maxval=3.0)
    window_width = jnp.exp(jax.random.uniform(number_of_pieces[4], (ATTENTION_GROUPS, SEQUENCE_STEPS // GROUP, 1), minval=math.log(0.5), maxval=math.log(2.0)))
    window_width = jnp.broadcast_to(window_width, (ATTENTION_GROUPS, SEQUENCE_STEPS // GROUP, GROUP)).reshape(ATTENTION_GROUPS, SEQUENCE_STEPS)
    segment_extent = jax.random.uniform(number_of_pieces[5], (ATTENTION_GROUPS, SEQUENCE_STEPS)) < 3.0 / SEQUENCE_STEPS
    sequence_steps_total = jax.random.uniform(number_of_pieces[6], (ATTENTION_GROUPS, SEQUENCE_STEPS), minval=0.22, maxval=0.69)
    return (-(starting_position * approximate_guess * window_width + jnp.where(segment_extent, sequence_steps_total, 0.0))).astype(jnp.float32)


def place_ends(entries, rng, least, top_value):
    longest = entries.shape.index(max(entries.shape))
    spots = []
    for shift in (0, 1):
        where = [jax.random.randint(jax.random.fold_in(rng, axis), (), 0, length) for axis, length in enumerate(entries.shape)]
        where[longest] = (where[longest] + shift) % entries.shape[longest]
        spots.append(tuple(where))
    return entries.at[spots[0]].set(least).at[spots[1]].set(top_value)


def level_of(own_key, dims, cuts, smallest, top_value):
    level, own = 1.0, jax.random.fold_in(own_key, 6)
    for axis_at, shards_of in cuts:
        steps = jnp.exp(jax.random.uniform(jax.random.fold_in(own, axis_at), (shards_of,), jnp.float32, smallest / len(cuts), top_value / len(cuts)))
        level = level * jnp.repeat(steps, dims[axis_at] // shards_of).reshape([-1 if axis == axis_at else 1 for axis in range(len(dims))])
    return level


def noise(key, shape, width, reach, pieces=(), dtype=jnp.bfloat16):
    loudness = level_of(key, shape, pieces, -0.22, 0.18) if pieces else 1.0
    array = jax.random.normal(key, shape, jnp.float32) * width * loudness
    return jnp.minimum(jnp.maximum(array, -reach), reach).astype(dtype)


def setup_inputs(seed: int = 0) -> dict:
    seeds = jax.random.split(jax.random.key(seed), 8)
    return {
        "queries": noise(seeds[0], (SEQUENCE_STEPS, WIDTH), 1.0, 6.0, ((0, 64), (1, 8))),
        "keys": noise(seeds[1], (SEQUENCE_STEPS, WIDTH), 1.0, 6.0, ((0, 64), (1, 8))),
        "values": noise(seeds[2], (SEQUENCE_STEPS, WIDTH), 1.0, 6.0, ((0, 64), (1, 8))),
        "log_decay": draw_log_decay(jax.random.fold_in(seeds[7], 71), 0),
        "agent_ids": place_ends(jax.random.randint(seeds[4], (SEQUENCE_STEPS,), 0, AGENTS), jax.random.fold_in(seeds[4], 1), 0, AGENTS - 1).astype(jnp.int32),
        "norm_gain": jnp.clip(1.0 + 0.18 * jax.random.normal(seeds[5], (WIDTH,), jnp.float32), 0.1, 1.9),
        "out_grad": noise(seeds[6], (SEQUENCE_STEPS, WIDTH), 1.0, 6.0, ((0, 64), (1, 8))),
    }


EPS = 1e-06
HIGH = lax.Precision.HIGHEST

def group_pass(scaled, key_rows, value_rows, decays, teams):
    length, heads, depth = scaled.shape
    blocks = length // GROUP
    query_blocks = scaled.reshape(blocks, GROUP, heads, depth)
    key_blocks = key_rows.reshape(blocks, GROUP, heads, depth)
    value_blocks = value_rows.reshape(blocks, GROUP, heads, depth)
    decay_blocks = decays.reshape(heads, blocks, GROUP).transpose(1, 0, 2)
    team_blocks = teams.reshape(blocks, GROUP)
    places = jnp.arange(GROUP)
    causal = places[:, None] >= places[None, :]

    def advance(state, inputs):
        query_block, key_block, value_block, decay_block, team_block = inputs
        cumulative = jnp.cumsum(decay_block, axis=1)
        visible = (causal & (team_block[:, None] == team_block[None, :]))[None]
        spread = cumulative[:, :, None] - cumulative[:, None, :]
        weights = jnp.where(visible, jnp.exp(jnp.where(visible, spread, 0.0)), 0.0)
        scores = jnp.einsum('thd,shd->hts', query_block, key_block, precision=HIGH) * weights
        output = jnp.einsum('hts,she->the', scores, value_block, precision=HIGH)
        carried = jnp.einsum('thd,hde->the', query_block, state, precision=HIGH)
        output = output + jnp.exp(cumulative).T[:, :, None] * carried
        tail = jnp.exp(cumulative[:, -1:] - cumulative)
        fresh = jnp.einsum('shd,she->hde', key_block * tail.T[:, :, None], value_block, precision=HIGH)
        state = jnp.exp(cumulative[:, -1])[:, None, None] * state + fresh
        return (state, output)
    start = jnp.zeros((heads, depth, depth), jnp.float32)
    final, outputs = lax.scan(advance, start, (query_blocks, key_blocks, value_blocks, decay_blocks, team_blocks))
    return (outputs.reshape(length, heads, depth), final)

def layer(query_in, key_in, value_in, decays, gain, teams):
    length = query_in.shape[0]
    scaled = query_in.reshape(length, ATTENTION_GROUPS, DK) * DK ** (-0.5)
    output, final = group_pass(scaled, key_in.reshape(length, ATTENTION_GROUPS, DK), value_in.reshape(length, ATTENTION_GROUPS, DK), decays, teams)
    flat = output.reshape(length, WIDTH)
    rms_value = jnp.sqrt(lax.optimization_barrier(jnp.mean(flat * flat, axis=1)) + EPS)
    return flat / rms_value[:, None] * gain

def reference(queries, keys, values, log_decay, agent_ids, norm_gain, out_grad):
    teams = agent_ids // TEAM

    def forward(query_in, key_in, value_in, decays, gain):
        return layer(query_in, key_in, value_in, decays, gain, teams)
    output, pullback = jax.vjp(forward, queries.astype(jnp.float32), keys.astype(jnp.float32), values.astype(jnp.float32), log_decay, norm_gain)
    query_g, key_g, value_g, decay_g, gain_g = pullback(out_grad.astype(jnp.float32))
    return (output.astype(jnp.bfloat16), query_g.astype(jnp.bfloat16), key_g.astype(jnp.bfloat16), value_g.astype(jnp.bfloat16), decay_g, gain_g)
```

```python
import functools

import jax
import jax.numpy as jnp
from jax import lax
from jax.experimental import pallas as pl
from jax.experimental.pallas import tpu as pltpu
from jax.sharding import PartitionSpec as P

DK = 128
STEPS = 128
HEADS = 4
TEAM = 16
WIDTH = 4096
EPS = 1e-06
SCALE = DK ** (-0.5)
Z = 16
Y = 4
ROWS = HEADS * DK // Z
F32 = jnp.float32
BF16 = jnp.bfloat16

NN = (((1,), (0,)), ((), ()))
NT = (((1,), (1,)), ((), ()))
TN = (((0,), (0,)), ((), ()))


def mm(a, b, dims):
    return lax.dot_general(a, b, dims, preferred_element_type=F32)


def exact(a, b, dims):
    return lax.dot_general(
        a, b, dims, precision=lax.Precision.HIGHEST, preferred_element_type=F32
    )


def parts(a):
    high = a.astype(BF16)
    return high, (a - high.astype(F32)).astype(BF16)


def wide_left(a, b, dims):
    high, low = parts(a)
    return mm(high, b, dims) + mm(low, b, dims)


def wide_right(a, b, dims):
    high, low = parts(b)
    return mm(a, high, dims) + mm(a, low, dims)


def wide_both(a, b, dims):
    ah, al = parts(a)
    bh, bl = parts(b)
    return mm(ah, bh, dims) + (mm(ah, bl, dims) + mm(al, bh, dims))


def grid_index():
    rows = lax.broadcasted_iota(jnp.int32, (STEPS, STEPS), 0)
    cols = lax.broadcasted_iota(jnp.int32, (STEPS, STEPS), 1)
    return rows, cols


def head(ref, h):
    return ref[:, h * DK : (h + 1) * DK]


def state_kernel(k_ref, v_ref, decay_ref, out_ref):
    rows, cols = grid_index()
    decay = decay_ref[...]
    after = exact((cols > rows).astype(F32), decay, NT)
    tail = jnp.exp(after)
    factor = jnp.exp(jnp.sum(decay, axis=1, keepdims=True))
    for h in range(HEADS):
        k = head(k_ref, h).astype(F32) * tail[:, h : h + 1]
        state = wide_left(k, head(v_ref, h), TN)
        for j in range(Z // HEADS):
            out_ref[h * (Z // HEADS) + j, :ROWS, :] = state[j * ROWS : (j + 1) * ROWS]
            out_ref[h * (Z // HEADS) + j, ROWS:, :] = jnp.broadcast_to(factor[h : h + 1], (8, DK))


def tiled(factor, value):
    return (value.reshape(ROWS // 8, 8, DK) * factor[None]).reshape(ROWS, DK)


def row_scan_kernel(backward, with_gain, *refs):
    if with_gain:
        in_ref, factor_ref, gain_ref, local_ref, row_ref = refs
    else:
        in_ref, local_ref, reach_ref, factor_ref, row_ref = refs
    order = range(Z - 1, -1, -1) if backward else range(Z)
    running = jnp.zeros((ROWS, DK), F32)
    product = jnp.ones((8, DK), F32)
    for z in order:
        factor = factor_ref[z] if with_gain else in_ref[z, ROWS:, :]
        local_ref[z] = running
        if not with_gain:
            reach_ref[z] = product
            factor_ref[z] = factor
        running = tiled(factor, running) + in_ref[z, :ROWS, :]
        product = product * factor
    extra = gain_ref[...] if with_gain else product
    for y in range(Y):
        row_ref[y, :ROWS, :] = running
        row_ref[y, ROWS:, :] = extra


def join_kernel(backward, with_gain, *refs):
    if with_gain:
        in_ref, local_ref, factor_ref, rows_ref, out_ref = refs
    else:
        in_ref, local_ref, reach_ref, out_ref = refs
    mine = lax.axis_index("tm") // Z
    running = jnp.zeros((ROWS, DK), F32)
    order = range(Y - 1, 0, -1) if backward else range(Y - 1)
    for y in order:
        factor = rows_ref[y, ROWS:, :] if with_gain else in_ref[y, ROWS:, :]
        longer = tiled(factor, running) + in_ref[y, :ROWS, :]
        use = (y > mine) if backward else (y < mine)
        running = jnp.where(use, longer, running)
    if with_gain:
        gain = in_ref[0, ROWS:, :]
        for y in range(1, Y):
            gain = gain + in_ref[y, ROWS:, :]
        product = jnp.ones((8, DK), F32)
        for z in range(Z - 1, -1, -1):
            out_ref[z, :ROWS, :] = local_ref[z] + tiled(product, running)
            out_ref[z, ROWS:, :] = gain
            product = product * factor_ref[z]
    else:
        for z in range(Z):
            out_ref[z] = local_ref[z] + tiled(reach_ref[z], running)


def decays(decay):
    rows, cols = grid_index()
    lower = (cols <= rows).astype(F32)
    column = exact(lower, decay, NT)
    row = exact(decay, lower, NT)
    return column, row


def weights_of(column, row, visible, h):
    spread = column[:, h : h + 1] - row[h : h + 1, :]
    return jnp.where(visible, jnp.exp(jnp.where(visible, spread, 0.0)), 0.0)


def visible_of(ids_ref):
    rows, cols = grid_index()
    team = jnp.broadcast_to((ids_ref[...] // TEAM).astype(F32), (STEPS, STEPS))
    return (cols <= rows) & (team == team.T)


def state_of(ref, h):
    per = Z // HEADS
    return jnp.concatenate([ref[h * per + j, :ROWS, :] for j in range(per)], axis=0)


def output_kernel(q_ref, k_ref, v_ref, decay_ref, ids_ref, gain_ref, grad_ref, state_ref, out_ref, sums_ref):
    column, row = decays(decay_ref[...])
    visible = visible_of(ids_ref)
    grown = jnp.exp(column)
    squares = jnp.zeros((STEPS, DK), F32)
    inners = jnp.zeros((STEPS, DK), F32)
    for h in range(HEADS):
        q, k, v = head(q_ref, h), head(k_ref, h), head(v_ref, h)
        scores = mm(q, k, NT) * (weights_of(column, row, visible, h) * SCALE)
        inter = wide_right(q, state_of(state_ref, h), NN)
        out = wide_left(scores, v, NN) + (grown[:, h : h + 1] * SCALE) * inter
        out_ref[:, h * DK : (h + 1) * DK] = out
        squares = squares + out * out
        inners = inners + head(grad_ref, h).astype(F32) * head(gain_ref, h) * out
    ones = jnp.ones((8, DK), F32)
    both = jnp.where(
        lax.broadcasted_iota(jnp.int32, (8, STEPS), 0) == 0,
        exact(ones, squares, NT),
        exact(ones, inners, NT),
    )
    for p in range(8):
        sums_ref[p] = both


def norm_kernel(sums_ref, o_ref, q_ref, decay_ref, gain_ref, grad_ref, result_ref, adjoint_ref, own_ref, part_ref):
    rows, cols = grid_index()
    total = sums_ref[0]
    for p in range(1, 8):
        total = total + sums_ref[p]
    total = total.T
    inverse = 1.0 / jnp.sqrt(total[:, 0:1] / WIDTH + EPS)
    pull = total[:, 1:2] * (inverse * inverse * inverse) / WIDTH
    grown = jnp.exp(exact((cols <= rows).astype(F32), decay_ref[...], NT)) * SCALE
    part_ref[...] = jnp.zeros((8, DK), F32)
    for h in range(HEADS):
        out = head(o_ref, h)
        gain = head(gain_ref, h)
        grad = head(grad_ref, h).astype(F32)
        normed = out * inverse
        result_ref[:, h * DK : (h + 1) * DK] = (normed * gain).astype(BF16)
        part_ref[h : h + 1, :] = jnp.sum(grad * normed, axis=0, keepdims=True)
        adjoint = grad * gain * inverse - out * pull
        adjoint_ref[:, h * DK : (h + 1) * DK] = adjoint
        own = wide_right(head(q_ref, h), adjoint * grown[:, h : h + 1], TN)
        for j in range(Z // HEADS):
            own_ref[h * (Z // HEADS) + j] = own[j * ROWS : (j + 1) * ROWS]


def final_kernel(
    q_ref, k_ref, v_ref, decay_ref, ids_ref, state_ref, adjoint_ref, end_ref,
    dq_ref, dk_ref, dv_ref, dd_ref, dg_ref,
):
    decay = decay_ref[...]
    column, row = decays(decay)
    rows, cols = grid_index()
    visible = visible_of(ids_ref)
    grown = jnp.exp(column)
    tail = jnp.exp(exact((cols > rows).astype(F32), decay, NT))
    factor = jnp.exp(jnp.sum(decay, axis=1, keepdims=True))
    until = (rows >= cols).astype(F32)
    before = (rows < cols).astype(F32)
    for h in range(HEADS):
        span = slice(h * DK, (h + 1) * DK)
        q, k, v = head(q_ref, h), head(k_ref, h), head(v_ref, h)
        adjoint = head(adjoint_ref, h)
        state = state_of(state_ref, h)
        end = state_of(end_ref, h)
        weights = weights_of(column, row, visible, h) * SCALE
        scores = mm(q, k, NT) * weights
        slopes = wide_left(adjoint, v, NT)
        joint = scores * slopes
        slopes = slopes * weights
        inter = wide_both(adjoint, state, NT) * (grown[:, h : h + 1] * SCALE)
        dq_ref[:, span] = (wide_left(slopes, k, NN) + inter).astype(BF16)
        dk_end = wide_right(v, end, NT) * tail[:, h : h + 1]
        dk_ref[:, span] = (wide_left(slopes, q, TN) + dk_end).astype(BF16)
        dv_end = wide_right(k, end, NN) * tail[:, h : h + 1]
        dv_ref[:, span] = (wide_both(scores, adjoint, TN) + dv_end).astype(BF16)
        late = jnp.sum(joint + inter * q.astype(F32), axis=1, keepdims=True)
        early = jnp.sum(dk_end * k.astype(F32), axis=1, keepdims=True)
        columns = jnp.sum(joint, axis=0, keepdims=True)
        through = factor[h : h + 1] * jnp.sum(end * state)
        dd_ref[h : h + 1, :] = (
            jnp.sum(late * until, axis=0, keepdims=True)
            + jnp.sum(early * before, axis=0, keepdims=True)
            - exact(jnp.broadcast_to(columns, (8, STEPS)), until, NN)[0:1]
            + through
        )
    total = end_ref[0, ROWS:, :]
    for z in range(1, Z):
        total = total + end_ref[z, ROWS:, :]
    dg_ref[...] = total


def call(kernel, shapes, *arrays):
    return pl.pallas_call(
        kernel,
        out_shape=[jax.ShapeDtypeStruct(s, d) for s, d in shapes],
        in_specs=[pl.BlockSpec(memory_space=pltpu.VMEM)] * len(arrays),
        out_specs=[pl.BlockSpec(memory_space=pltpu.VMEM)] * len(shapes),
    )(*arrays)


Z_GROUPS = [[y * Z + z for z in range(Z)] for y in range(Y)]
Y_GROUPS = [[y * Z + z for y in range(Y)] for z in range(Z)]


def swap(value, axis, groups=None):
    return lax.all_to_all(value, axis, 0, 0, axis_index_groups=groups, tiled=True)


def body(queries, keys, values, log_decay, agent_ids, norm_gain, out_grad):
    ids = agent_ids.reshape(1, STEPS)
    gain = norm_gain.reshape(1, HEADS * DK)
    wide = (STEPS, HEADS * DK)
    slices, padded = (Z, ROWS, DK), (Z, ROWS + 8, DK)
    (ends,) = call(state_kernel, [(padded, F32)], keys, values, log_decay)
    ends = swap(ends, "tm", Z_GROUPS)
    local, reach, factors, row = call(
        functools.partial(row_scan_kernel, False, False),
        [(slices, F32), ((Z, 8, DK), F32), ((Z, 8, DK), F32), ((Y, ROWS + 8, DK), F32)],
        ends,
    )
    rows = swap(row, "tm", Y_GROUPS)
    (entering,) = call(functools.partial(join_kernel, False, False), [(slices, F32)], rows, local, reach)
    state = swap(entering, "tm", Z_GROUPS)
    out, sums = call(
        output_kernel,
        [(wide, F32), ((8, 8, STEPS), F32)],
        queries, keys, values, log_decay, ids, gain, out_grad, state,
    )
    sums = swap(sums, "head")
    result, adjoint, own, part = call(
        norm_kernel,
        [(wide, BF16), (wide, F32), (slices, F32), ((8, DK), F32)],
        sums, out, queries, log_decay, gain, out_grad,
    )
    own = swap(own, "tm", Z_GROUPS)
    local, row = call(
        functools.partial(row_scan_kernel, True, True),
        [(slices, F32), ((Y, ROWS + 8, DK), F32)],
        own, factors, part,
    )
    row = swap(row, "tm", Y_GROUPS)
    (leaving,) = call(functools.partial(join_kernel, True, True), [(padded, F32)], row, local, factors, rows)
    end = swap(leaving, "tm", Z_GROUPS)
    query_grad, key_grad, value_grad, decay_grad, gain_grad = call(
        final_kernel,
        [(wide, BF16), (wide, BF16), (wide, BF16), ((HEADS, STEPS), F32), ((8, DK), F32)],
        queries, keys, values, log_decay, ids, state, adjoint, end,
    )
    return result, query_grad, key_grad, value_grad, decay_grad, gain_grad[:HEADS].reshape(-1)


def solution(mesh):
    wide = P("tm", "head")
    return jax.shard_map(
        body,
        mesh=mesh,
        in_specs=(wide, wide, wide, P("head", "tm"), P("tm"), P("head"), wide),
        out_specs=(wide, wide, wide, wide, P("head", "tm"), P("head")),
        check_vma=False,
    )
```

```python
import jax
import jax.numpy as jnp
from jax import lax
from jax.experimental import pallas as pl
from jax.experimental.pallas import tpu as pltpu
from jax.sharding import PartitionSpec as P

DK = 128
STEPS = 128
HEADS = 4
TEAM = 16
WIDTH = 4096
EPS = 1e-06
SCALE = DK ** (-0.5)
Z = 16
Y = 4
OWNERS = Z // HEADS
ROWS = DK // OWNERS
PACKED = ROWS + 1
MESSAGE = ROWS + 2
F32 = jnp.float32
BF16 = jnp.bfloat16

NN = (((1,), (0,)), ((), ()))
NT = (((1,), (1,)), ((), ()))
TN = (((0,), (0,)), ((), ()))


def mm(a, b, dims):
    return lax.dot_general(a, b, dims, preferred_element_type=F32)


def exact(a, b, dims):
    return lax.dot_general(
        a, b, dims, precision=lax.Precision.HIGHEST, preferred_element_type=F32
    )


def parts(a):
    high = a.astype(BF16)
    return high, (a - high.astype(F32)).astype(BF16)


def wide_left(a, b, dims):
    high, low = parts(a)
    return mm(high, b, dims) + mm(low, b, dims)


def wide_right(a, b, dims):
    high, low = parts(b)
    return mm(a, high, dims) + mm(a, low, dims)


def wide_both(a, b, dims):
    ah, al = parts(a)
    bh, bl = parts(b)
    return mm(ah, bh, dims) + (mm(ah, bl, dims) + mm(al, bh, dims))


def grid_index():
    rows = lax.broadcasted_iota(jnp.int32, (STEPS, STEPS), 0)
    cols = lax.broadcasted_iota(jnp.int32, (STEPS, STEPS), 1)
    return rows, cols


def head(ref, h):
    return ref[:, h * DK : (h + 1) * DK]


def slot(h, j):
    return (h * OWNERS + j) * PACKED


def spread_out(out_ref, h, state, row):
    for j in range(OWNERS):
        at = slot(h, j)
        out_ref[at : at + ROWS, :] = state[j * ROWS : (j + 1) * ROWS]
        out_ref[at + ROWS : at + PACKED, :] = row


def state_kernel(k_hbm, v_hbm, decay_hbm, out_hbm, k_ref, v_ref, decay_ref, out_ref, sems):
    loads = [
        pltpu.make_async_copy(source, target, sems.at[i])
        for i, (source, target) in enumerate(
            ((decay_hbm, decay_ref), (k_hbm, k_ref), (v_hbm, v_ref))
        )
    ]
    for load in loads:
        load.start()
    loads[0].wait()
    rows, cols = grid_index()
    decay = decay_ref[...]
    tail = jnp.exp(exact((cols > rows).astype(F32), decay, NT))
    factor = jnp.exp(jnp.sum(decay, axis=1, keepdims=True))
    loads[1].wait()
    loads[2].wait()
    stores = []
    for h in range(HEADS):
        k = head(k_ref, h).astype(F32) * tail[:, h : h + 1]
        state = wide_left(k, head(v_ref, h), TN)
        spread_out(out_ref, h, state, jnp.broadcast_to(factor[h : h + 1], (1, DK)))
        if h % 2:
            span = pl.ds(slot(h - 1, 0), 2 * OWNERS * PACKED)
            store = pltpu.make_async_copy(out_ref.at[span], out_hbm.at[span], sems.at[3 + h // 2])
            store.start()
            stores.append(store)
    for store in stores:
        store.wait()


def row_scan_kernel(in_ref, local_ref, factor_ref, reach_ref, row_ref):
    running = jnp.zeros((ROWS, DK), F32)
    product = jnp.ones((1, DK), F32)
    for z in range(Z):
        at = z * PACKED
        local_ref[z * ROWS : (z + 1) * ROWS, :] = running
        reach_ref[z : z + 1, :] = product
        factor = in_ref[at + ROWS : at + PACKED, :]
        factor_ref[z : z + 1, :] = factor
        running = factor * running + in_ref[at : at + ROWS, :]
        product = factor * product
    for y in range(Y):
        row_ref[y * MESSAGE : y * MESSAGE + ROWS, :] = running
        row_ref[y * MESSAGE + ROWS : (y + 1) * MESSAGE, :] = jnp.broadcast_to(product, (2, DK))


def join_kernel(rows_ref, local_ref, reach_ref, out_ref):
    mine = lax.axis_index("tm") // Z
    running = jnp.zeros((ROWS, DK), F32)
    for y in range(Y - 1):
        at = y * MESSAGE
        longer = rows_ref[at + ROWS : at + PACKED, :] * running + rows_ref[at : at + ROWS, :]
        running = jnp.where(y < mine, longer, running)
    for z in range(Z):
        span = slice(z * ROWS, (z + 1) * ROWS)
        out_ref[span, :] = local_ref[span, :] + reach_ref[z : z + 1, :] * running


def row_scan_back_kernel(in_ref, factor_ref, local_ref, row_ref):
    running = jnp.zeros((ROWS, DK), F32)
    gain = jnp.zeros((1, DK), F32)
    for z in range(Z - 1, -1, -1):
        at = z * PACKED
        local_ref[z * ROWS : (z + 1) * ROWS, :] = running
        running = factor_ref[z : z + 1, :] * running + in_ref[at : at + ROWS, :]
        gain = gain + in_ref[at + ROWS : at + PACKED, :]
    for y in range(Y):
        row_ref[y * MESSAGE : y * MESSAGE + ROWS, :] = running
        row_ref[y * MESSAGE + ROWS : (y + 1) * MESSAGE, :] = jnp.broadcast_to(gain, (2, DK))


def join_back_kernel(rows_ref, local_ref, factor_ref, totals_ref, out_ref):
    mine = lax.axis_index("tm") // Z
    running = jnp.zeros((ROWS, DK), F32)
    for y in range(Y - 1, 0, -1):
        at = y * MESSAGE
        longer = totals_ref[at + ROWS : at + PACKED, :] * running + rows_ref[at : at + ROWS, :]
        running = jnp.where(y > mine, longer, running)
    gain = rows_ref[ROWS:PACKED, :]
    for y in range(1, Y):
        gain = gain + rows_ref[y * MESSAGE + ROWS : y * MESSAGE + PACKED, :]
    product = jnp.ones((1, DK), F32)
    for z in range(Z - 1, -1, -1):
        at = z * PACKED
        out_ref[at : at + ROWS, :] = local_ref[z * ROWS : (z + 1) * ROWS, :] + product * running
        out_ref[at + ROWS : at + PACKED, :] = gain
        product = product * factor_ref[z : z + 1, :]


def decays(decay):
    rows, cols = grid_index()
    lower = (cols <= rows).astype(F32)
    column = exact(lower, decay, NT)
    row = exact(decay, lower, NT)
    return column, row


def weights_of(column, row, visible, h):
    spread = column[:, h : h + 1] - row[h : h + 1, :]
    return jnp.where(visible, jnp.exp(jnp.where(visible, spread, 0.0)), 0.0)


def visible_of(ids_ref):
    rows, cols = grid_index()
    team = jnp.broadcast_to((ids_ref[...] // TEAM).astype(F32), (STEPS, STEPS))
    return (cols <= rows) & (team == team.T)


def packed_state(ref, h):
    starts = [slot(h, j) for j in range(OWNERS)]
    return jnp.concatenate([ref[at : at + ROWS, :] for at in starts], axis=0)


def local_kernel(
    q_ref, k_ref, v_ref, decay_ref, ids_ref, gain_ref, grad_ref,
    scores_ref, weights_ref, out_ref, pull_ref, scales_ref, factor_ref,
):
    decay = decay_ref[...]
    column, row = decays(decay)
    rows, cols = grid_index()
    visible = visible_of(ids_ref)
    scales_ref[...] = jnp.zeros((STEPS, DK), F32)
    scales_ref[:, 0:HEADS] = jnp.exp(column) * SCALE
    scales_ref[:, HEADS : 2 * HEADS] = jnp.exp(exact((cols > rows).astype(F32), decay, NT))
    factor_ref[...] = jnp.broadcast_to(jnp.exp(jnp.sum(decay, axis=1, keepdims=True)), (HEADS, DK))
    for h in range(HEADS):
        span = slice(h * DK, (h + 1) * DK)
        weights = weights_of(column, row, visible, h) * SCALE
        scores = mm(head(q_ref, h), head(k_ref, h), NT) * weights
        weights_ref[:, span] = weights
        scores_ref[:, span] = scores
        out_ref[:, span] = wide_left(scores, head(v_ref, h), NN)
        pull_ref[:, span] = head(grad_ref, h).astype(F32) * head(gain_ref, h)


def grown_of(scales_ref, h):
    return scales_ref[:, h : h + 1]


def tail_of(scales_ref, h):
    return scales_ref[:, HEADS + h : HEADS + h + 1]


def output_kernel(q_ref, scales_ref, pull_ref, near_ref, state_ref, out_ref, sums_ref):
    squares = jnp.zeros((STEPS, DK), F32)
    inners = jnp.zeros((STEPS, DK), F32)
    for h in range(HEADS):
        span = slice(h * DK, (h + 1) * DK)
        inter = wide_right(head(q_ref, h), state_ref[span, :], NN)
        out = head(near_ref, h) + grown_of(scales_ref, h) * inter
        out_ref[:, span] = out
        squares = squares + out * out
        inners = inners + head(pull_ref, h) * out
    ones = jnp.ones((8, DK), F32)
    both = jnp.where(
        lax.broadcasted_iota(jnp.int32, (8, STEPS), 0) == 0,
        exact(ones, squares, NT),
        exact(ones, inners, NT),
    )
    for p in range(8):
        sums_ref[p] = both


def norm_kernel(sums_ref, o_ref, q_ref, scales_ref, pull_ref, grad_ref, adjoint_ref, inverse_ref, own_ref):
    total = sums_ref[0]
    for p in range(1, 8):
        total = total + sums_ref[p]
    inverse = 1.0 / jnp.sqrt(total[0:1] / WIDTH + EPS)
    back = total[1:2] * (inverse * inverse * inverse) / WIDTH
    both = jnp.concatenate([inverse, back, jnp.zeros((6, STEPS), F32)], axis=0).T
    inverse, back = both[:, 0:1], both[:, 1:2]
    inverse_ref[...] = jnp.broadcast_to(inverse, (STEPS, DK))
    for h in range(HEADS):
        out = head(o_ref, h)
        part = jnp.sum(head(grad_ref, h).astype(F32) * (out * inverse), axis=0, keepdims=True)
        adjoint = head(pull_ref, h) * inverse - out * back
        adjoint_ref[:, h * DK : (h + 1) * DK] = adjoint
        own = wide_right(head(q_ref, h), adjoint * grown_of(scales_ref, h), TN)
        spread_out(own_ref, h, own, part)


def local_back_kernel(
    q_ref, k_ref, v_ref, scales_ref, gain_ref, scores_ref, weights_ref, o_ref, inverse_ref, state_ref, adjoint_ref,
    result_ref, dq_ref, dk_ref, dv_ref, dd_ref,
):
    rows, cols = grid_index()
    until = (rows >= cols).astype(F32)
    inverse = inverse_ref[...]
    for h in range(HEADS):
        span = slice(h * DK, (h + 1) * DK)
        q, k, v = head(q_ref, h), head(k_ref, h), head(v_ref, h)
        result_ref[:, span] = (head(o_ref, h) * inverse * head(gain_ref, h)).astype(BF16)
        adjoint = head(adjoint_ref, h)
        scores = head(scores_ref, h)
        slopes = wide_left(adjoint, v, NT)
        joint = scores * slopes
        slopes = slopes * head(weights_ref, h)
        inter = wide_both(adjoint, state_ref[span, :], NT) * grown_of(scales_ref, h)
        dq_ref[:, span] = (wide_left(slopes, k, NN) + inter).astype(BF16)
        dk_ref[:, span] = wide_left(slopes, q, TN)
        dv_ref[:, span] = wide_both(scores, adjoint, TN)
        late = jnp.sum(joint + inter * q.astype(F32), axis=1, keepdims=True)
        columns = jnp.sum(joint, axis=0, keepdims=True)
        dd_ref[h : h + 1, :] = (
            jnp.sum(late * until, axis=0, keepdims=True)
            - exact(jnp.broadcast_to(columns, (8, STEPS)), until, NN)[0:1]
        )


def final_kernel(
    k_ref, v_ref, scales_ref, factor_ref, state_ref, near_dk_ref, near_dv_ref, near_dd_ref, end_ref,
    dk_ref, dv_ref, dd_ref, dg_ref,
):
    rows, cols = grid_index()
    before = (rows < cols).astype(F32)
    for h in range(HEADS):
        span = slice(h * DK, (h + 1) * DK)
        k, v = head(k_ref, h), head(v_ref, h)
        end = packed_state(end_ref, h)
        dk_end = wide_right(v, end, NT) * tail_of(scales_ref, h)
        dk_ref[:, span] = (head(near_dk_ref, h) + dk_end).astype(BF16)
        dv_end = wide_right(k, end, NN) * tail_of(scales_ref, h)
        dv_ref[:, span] = (head(near_dv_ref, h) + dv_end).astype(BF16)
        early = jnp.sum(dk_end * k.astype(F32), axis=1, keepdims=True)
        through = factor_ref[h : h + 1, :] * jnp.sum(end * state_ref[span, :])
        dd_ref[h : h + 1, :] = near_dd_ref[h : h + 1, :] + jnp.sum(early * before, axis=0, keepdims=True) + through
        dg_ref[:, span] = end_ref[slot(h, 0) + ROWS : slot(h, 0) + PACKED, :]


VMEM = pl.BlockSpec(memory_space=pltpu.VMEM)


def call(kernel, shapes, *arrays, specs=None, outs=None, scratch=(), cost=None, limit=16):
    return pl.pallas_call(
        kernel,
        out_shape=[jax.ShapeDtypeStruct(s, d) for s, d in shapes],
        in_specs=specs or [VMEM] * len(arrays),
        out_specs=outs or [VMEM] * len(shapes),
        scratch_shapes=list(scratch),
        cost_estimate=cost,
        compiler_params=pltpu.CompilerParams(vmem_limit_bytes=limit * 1024 * 1024),
    )(*arrays)


Z_GROUPS = [[y * Z + z for z in range(Z)] for y in range(Y)]
Y_GROUPS = [[y * Z + z for y in range(Y)] for z in range(Z)]


def exchange(value, groups, rows):
    peers = value.shape[0] // rows
    moved = lax.all_to_all(
        value.reshape(peers, rows, 1, DK), "tm", 0, 0, axis_index_groups=groups, tiled=True
    )
    return moved.reshape(value.shape)


def after(value, *others):
    return lax.optimization_barrier((value, *others))[0]


def body(queries, keys, values, log_decay, agent_ids, norm_gain, out_grad):
    ids = agent_ids.reshape(1, STEPS)
    gain = norm_gain.reshape(1, HEADS * DK)
    wide = (STEPS, HEADS * DK)
    plain, packed, totals = (Z * ROWS, DK), (Z * PACKED, DK), (Y * MESSAGE, DK)
    few = (Z, DK)
    long_cost = pl.CostEstimate(flops=40_000_000, bytes_accessed=2_000_000, transcendentals=65536)
    hbm = pl.BlockSpec(memory_space=pl.ANY)
    (ends,) = call(
        state_kernel, [(packed, F32)], keys, values, log_decay,
        specs=[hbm] * 3,
        outs=[hbm],
        scratch=[
            pltpu.VMEM(wide, BF16),
            pltpu.VMEM(wide, BF16),
            pltpu.VMEM((HEADS, STEPS), F32),
            pltpu.VMEM(packed, F32),
            pltpu.SemaphoreType.DMA((5,)),
        ],
        limit=60,
    )
    scores, weights, near, pull, scales, factor = call(
        local_kernel,
        [(wide, F32)] * 4 + [((STEPS, DK), F32), ((HEADS, DK), F32)],
        queries, keys, values, log_decay, ids, gain, out_grad,
        cost=long_cost,
    )
    ends = exchange(ends, Z_GROUPS, PACKED)
    local, factors, reach, row = call(
        row_scan_kernel, [(plain, F32), (few, F32), (few, F32), (totals, F32)], ends
    )
    rows = exchange(after(row, near), Y_GROUPS, MESSAGE)
    (entering,) = call(join_kernel, [(plain, F32)], rows, local, reach)
    state = exchange(entering, Z_GROUPS, ROWS)
    out, sums = call(
        output_kernel,
        [(wide, F32), ((8, 8, STEPS), F32)],
        queries, scales, pull, near, state,
    )
    sums = lax.all_to_all(sums, "head", 0, 0, tiled=True)
    adjoint, inverse, own = call(
        norm_kernel,
        [(wide, F32), ((STEPS, DK), F32), (packed, F32)],
        sums, out, queries, scales, pull, out_grad,
    )
    result, query_grad, near_dk, near_dv, near_dd = call(
        local_back_kernel,
        [(wide, BF16), (wide, BF16), (wide, F32), (wide, F32), ((HEADS, STEPS), F32)],
        queries, keys, values, scales, gain, scores, weights, out, inverse, state, adjoint,
        cost=long_cost,
    )
    own = exchange(own, Z_GROUPS, PACKED)
    local, row = call(row_scan_back_kernel, [(plain, F32), (totals, F32)], own, factors)
    row = exchange(row, Y_GROUPS, MESSAGE)
    (leaving,) = call(join_back_kernel, [(packed, F32)], row, local, factors, rows)
    end = exchange(leaving, Z_GROUPS, PACKED)
    key_grad, value_grad, decay_grad, gain_grad = call(
        final_kernel,
        [(wide, BF16), (wide, BF16), ((HEADS, STEPS), F32), ((1, HEADS * DK), F32)],
        keys, values, scales, factor, state, near_dk, near_dv, near_dd, end,
    )
    return result, query_grad, key_grad, value_grad, decay_grad, gain_grad.reshape(-1)


def solution(mesh):
    wide = P("tm", "head")
    return jax.shard_map(
        body,
        mesh=mesh,
        in_specs=(wide, wide, wide, P("head", "tm"), P("tm"), P("head"), wide),
        out_specs=(wide, wide, wide, wide, P("head", "tm"), P("head")),
        check_vma=False,
    )
```

```python
import jax
import jax.numpy as jnp
from jax import lax
from jax.experimental import pallas as pl
from jax.experimental.pallas import tpu as pltpu
from jax.sharding import PartitionSpec as P

DK = 128
STEPS = 128
HEADS = 4
TEAM = 16
WIDTH = 4096
EPS = 1e-06
CORES = 2
STAGGER_NS = 4000
SCALE = DK ** (-0.5)
Z = 16
Y = 4
OWNERS = Z // HEADS
ROWS = DK // OWNERS
PACKED = ROWS + 1
MESSAGE = ROWS + 2
F32 = jnp.float32
BF16 = jnp.bfloat16

NN = (((1,), (0,)), ((), ()))
NT = (((1,), (1,)), ((), ()))
TN = (((0,), (0,)), ((), ()))


def mm(a, b, dims):
    return lax.dot_general(a, b, dims, preferred_element_type=F32)


def exact(a, b, dims):
    return lax.dot_general(
        a, b, dims, precision=lax.Precision.HIGHEST, preferred_element_type=F32
    )


def parts(a):
    high = a.astype(BF16)
    return high, (a - high.astype(F32)).astype(BF16)


def wide_left(a, b, dims):
    high, low = parts(a)
    return mm(high, b, dims) + mm(low, b, dims)


def wide_right(a, b, dims):
    high, low = parts(b)
    return mm(a, high, dims) + mm(a, low, dims)


def wide_both(a, b, dims):
    ah, al = parts(a)
    bh, bl = parts(b)
    return mm(ah, bh, dims) + (mm(ah, bl, dims) + mm(al, bh, dims))


def grid_index():
    rows = lax.broadcasted_iota(jnp.int32, (STEPS, STEPS), 0)
    cols = lax.broadcasted_iota(jnp.int32, (STEPS, STEPS), 1)
    return rows, cols


def head(ref, h):
    return ref[:, h * DK : (h + 1) * DK]


def slot(h, j):
    return (h * OWNERS + j) * PACKED


def spread_out(out_ref, h, state, row):
    for j in range(OWNERS):
        at = slot(h, j)
        out_ref[at : at + ROWS, :] = state[j * ROWS : (j + 1) * ROWS]
        out_ref[at + ROWS : at + PACKED, :] = row


def state_kernel(k_hbm, v_hbm, decay_hbm, out_hbm, k_ref, v_ref, decay_ref, out_ref, sems):
    loads = [
        pltpu.make_async_copy(source, target, sems.at[i])
        for i, (source, target) in enumerate(
            ((decay_hbm, decay_ref), (k_hbm, k_ref), (v_hbm, v_ref))
        )
    ]
    for load in loads:
        load.start()
    loads[0].wait()
    @pl.when(lax.axis_index("head") % CORES == 0)
    def _wait():
        pl.delay(STAGGER_NS)

    rows, cols = grid_index()
    decay = decay_ref[...]
    tail = jnp.exp(exact((cols > rows).astype(F32), decay, NT))
    factor = jnp.exp(jnp.sum(decay, axis=1, keepdims=True))
    loads[1].wait()
    loads[2].wait()
    stores = []
    for h in range(HEADS):
        k = head(k_ref, h).astype(F32) * tail[:, h : h + 1]
        state = wide_left(k, head(v_ref, h), TN)
        spread_out(out_ref, h, state, jnp.broadcast_to(factor[h : h + 1], (1, DK)))
        if h % 2:
            span = pl.ds(slot(h - 1, 0), 2 * OWNERS * PACKED)
            store = pltpu.make_async_copy(out_ref.at[span], out_hbm.at[span], sems.at[3 + h // 2])
            store.start()
            stores.append(store)
    for store in stores:
        store.wait()


def row_scan_kernel(in_ref, local_ref, factor_ref, reach_ref, row_ref):
    running = jnp.zeros((ROWS, DK), F32)
    product = jnp.ones((1, DK), F32)
    for z in range(Z):
        at = z * PACKED
        local_ref[z * ROWS : (z + 1) * ROWS, :] = running
        reach_ref[z : z + 1, :] = product
        factor = in_ref[at + ROWS : at + PACKED, :]
        factor_ref[z : z + 1, :] = factor
        running = factor * running + in_ref[at : at + ROWS, :]
        product = factor * product
    for y in range(Y):
        row_ref[y * MESSAGE : y * MESSAGE + ROWS, :] = running
        row_ref[y * MESSAGE + ROWS : (y + 1) * MESSAGE, :] = jnp.broadcast_to(product, (2, DK))


def join_kernel(rows_ref, local_ref, reach_ref, out_ref):
    mine = lax.axis_index("tm") // Z
    running = jnp.zeros((ROWS, DK), F32)
    for y in range(Y - 1):
        at = y * MESSAGE
        longer = rows_ref[at + ROWS : at + PACKED, :] * running + rows_ref[at : at + ROWS, :]
        running = jnp.where(y < mine, longer, running)
    for z in range(Z):
        span = slice(z * ROWS, (z + 1) * ROWS)
        out_ref[span, :] = local_ref[span, :] + reach_ref[z : z + 1, :] * running


def row_scan_back_kernel(in_ref, factor_ref, local_ref, row_ref):
    running = jnp.zeros((ROWS, DK), F32)
    gain = jnp.zeros((1, DK), F32)
    for z in range(Z - 1, -1, -1):
        at = z * PACKED
        local_ref[z * ROWS : (z + 1) * ROWS, :] = running
        running = factor_ref[z : z + 1, :] * running + in_ref[at : at + ROWS, :]
        gain = gain + in_ref[at + ROWS : at + PACKED, :]
    for y in range(Y):
        row_ref[y * MESSAGE : y * MESSAGE + ROWS, :] = running
        row_ref[y * MESSAGE + ROWS : (y + 1) * MESSAGE, :] = jnp.broadcast_to(gain, (2, DK))


def join_back_kernel(rows_ref, local_ref, factor_ref, totals_ref, out_ref):
    mine = lax.axis_index("tm") // Z
    running = jnp.zeros((ROWS, DK), F32)
    for y in range(Y - 1, 0, -1):
        at = y * MESSAGE
        longer = totals_ref[at + ROWS : at + PACKED, :] * running + rows_ref[at : at + ROWS, :]
        running = jnp.where(y > mine, longer, running)
    gain = rows_ref[ROWS:PACKED, :]
    for y in range(1, Y):
        gain = gain + rows_ref[y * MESSAGE + ROWS : y * MESSAGE + PACKED, :]
    product = jnp.ones((1, DK), F32)
    for z in range(Z - 1, -1, -1):
        at = z * PACKED
        out_ref[at : at + ROWS, :] = local_ref[z * ROWS : (z + 1) * ROWS, :] + product * running
        out_ref[at + ROWS : at + PACKED, :] = gain
        product = product * factor_ref[z : z + 1, :]


def decays(decay):
    rows, cols = grid_index()
    lower = (cols <= rows).astype(F32)
    column = exact(lower, decay, NT)
    row = exact(decay, lower, NT)
    return column, row


def weights_of(column, row, visible, h):
    spread = column[:, h : h + 1] - row[h : h + 1, :]
    return jnp.where(visible, jnp.exp(jnp.where(visible, spread, 0.0)), 0.0)


def visible_of(ids_ref):
    rows, cols = grid_index()
    team = jnp.broadcast_to((ids_ref[...] // TEAM).astype(F32), (STEPS, STEPS))
    return (cols <= rows) & (team == team.T)


def packed_state(ref, h):
    starts = [slot(h, j) for j in range(OWNERS)]
    return jnp.concatenate([ref[at : at + ROWS, :] for at in starts], axis=0)


def local_kernel(
    q_ref, k_ref, v_ref, decay_ref, ids_ref, gain_ref, grad_ref,
    scores_ref, weights_ref, out_ref, pull_ref, scales_ref, factor_ref,
):
    decay = decay_ref[...]
    column, row = decays(decay)
    rows, cols = grid_index()
    visible = visible_of(ids_ref)
    scales_ref[...] = jnp.zeros((STEPS, DK), F32)
    scales_ref[:, 0:HEADS] = jnp.exp(column) * SCALE
    scales_ref[:, HEADS : 2 * HEADS] = jnp.exp(exact((cols > rows).astype(F32), decay, NT))
    factor_ref[...] = jnp.broadcast_to(jnp.exp(jnp.sum(decay, axis=1, keepdims=True)), (HEADS, DK))
    for h in range(HEADS):
        span = slice(h * DK, (h + 1) * DK)
        weights = weights_of(column, row, visible, h) * SCALE
        scores = mm(head(q_ref, h), head(k_ref, h), NT) * weights
        weights_ref[:, span] = weights
        scores_ref[:, span] = scores
        out_ref[:, span] = wide_left(scores, head(v_ref, h), NN)
        pull_ref[:, span] = head(grad_ref, h).astype(F32) * head(gain_ref, h)


def grown_of(scales_ref, h):
    return scales_ref[:, h : h + 1]


def tail_of(scales_ref, h):
    return scales_ref[:, HEADS + h : HEADS + h + 1]


def output_kernel(q_ref, scales_ref, pull_ref, near_ref, state_ref, out_ref, sums_ref):
    squares = jnp.zeros((STEPS, DK), F32)
    inners = jnp.zeros((STEPS, DK), F32)
    for h in range(HEADS):
        span = slice(h * DK, (h + 1) * DK)
        inter = wide_right(head(q_ref, h), state_ref[span, :], NN)
        out = head(near_ref, h) + grown_of(scales_ref, h) * inter
        out_ref[:, span] = out
        squares = squares + out * out
        inners = inners + head(pull_ref, h) * out
    ones = jnp.ones((8, DK), F32)
    both = jnp.where(
        lax.broadcasted_iota(jnp.int32, (8, STEPS), 0) == 0,
        exact(ones, squares, NT),
        exact(ones, inners, NT),
    )
    for p in range(8):
        sums_ref[p] = both


def norm_kernel(sums_ref, o_ref, q_ref, scales_ref, pull_ref, grad_ref, adjoint_ref, inverse_ref, own_ref):
    @pl.when(lax.axis_index("head") % CORES == 0)
    def _wait():
        pl.delay(STAGGER_NS)

    total = sums_ref[0]
    for p in range(1, 8):
        total = total + sums_ref[p]
    inverse = 1.0 / jnp.sqrt(total[0:1] / WIDTH + EPS)
    back = total[1:2] * (inverse * inverse * inverse) / WIDTH
    both = jnp.concatenate([inverse, back, jnp.zeros((6, STEPS), F32)], axis=0).T
    inverse, back = both[:, 0:1], both[:, 1:2]
    inverse_ref[...] = jnp.broadcast_to(inverse, (STEPS, DK))
    for h in range(HEADS):
        out = head(o_ref, h)
        part = jnp.sum(head(grad_ref, h).astype(F32) * (out * inverse), axis=0, keepdims=True)
        adjoint = head(pull_ref, h) * inverse - out * back
        adjoint_ref[:, h * DK : (h + 1) * DK] = adjoint
        own = wide_right(head(q_ref, h), adjoint * grown_of(scales_ref, h), TN)
        spread_out(own_ref, h, own, part)


def local_back_kernel(
    q_ref, k_ref, v_ref, scales_ref, gain_ref, scores_ref, weights_ref, o_ref, inverse_ref, state_ref, adjoint_ref,
    result_ref, dq_ref, dk_ref, dv_ref, dd_ref,
):
    rows, cols = grid_index()
    until = (rows >= cols).astype(F32)
    inverse = inverse_ref[...]
    for h in range(HEADS):
        span = slice(h * DK, (h + 1) * DK)
        q, k, v = head(q_ref, h), head(k_ref, h), head(v_ref, h)
        result_ref[:, span] = (head(o_ref, h) * inverse * head(gain_ref, h)).astype(BF16)
        adjoint = head(adjoint_ref, h)
        scores = head(scores_ref, h)
        slopes = wide_left(adjoint, v, NT)
        joint = scores * slopes
        slopes = slopes * head(weights_ref, h)
        inter = wide_both(adjoint, state_ref[span, :], NT) * grown_of(scales_ref, h)
        dq_ref[:, span] = (wide_left(slopes, k, NN) + inter).astype(BF16)
        dk_ref[:, span] = wide_left(slopes, q, TN)
        dv_ref[:, span] = wide_both(scores, adjoint, TN)
        late = jnp.sum(joint + inter * q.astype(F32), axis=1, keepdims=True)
        columns = jnp.sum(joint, axis=0, keepdims=True)
        dd_ref[h : h + 1, :] = (
            jnp.sum(late * until, axis=0, keepdims=True)
            - exact(jnp.broadcast_to(columns, (8, STEPS)), until, NN)[0:1]
        )


def final_kernel(
    k_ref, v_ref, scales_ref, factor_ref, state_ref, near_dk_ref, near_dv_ref, near_dd_ref, end_ref,
    dk_ref, dv_ref, dd_ref, dg_ref,
):
    rows, cols = grid_index()
    before = (rows < cols).astype(F32)
    for h in range(HEADS):
        span = slice(h * DK, (h + 1) * DK)
        k, v = head(k_ref, h), head(v_ref, h)
        end = packed_state(end_ref, h)
        dk_end = wide_right(v, end, NT) * tail_of(scales_ref, h)
        dk_ref[:, span] = (head(near_dk_ref, h) + dk_end).astype(BF16)
        dv_end = wide_right(k, end, NN) * tail_of(scales_ref, h)
        dv_ref[:, span] = (head(near_dv_ref, h) + dv_end).astype(BF16)
        early = jnp.sum(dk_end * k.astype(F32), axis=1, keepdims=True)
        through = factor_ref[h : h + 1, :] * jnp.sum(end * state_ref[span, :])
        dd_ref[h : h + 1, :] = near_dd_ref[h : h + 1, :] + jnp.sum(early * before, axis=0, keepdims=True) + through
        dg_ref[:, span] = end_ref[slot(h, 0) + ROWS : slot(h, 0) + PACKED, :]


VMEM = pl.BlockSpec(memory_space=pltpu.VMEM)


def call(kernel, shapes, *arrays, specs=None, outs=None, scratch=(), cost=None, limit=16):
    return pl.pallas_call(
        kernel,
        out_shape=[jax.ShapeDtypeStruct(s, d) for s, d in shapes],
        in_specs=specs or [VMEM] * len(arrays),
        out_specs=outs or [VMEM] * len(shapes),
        scratch_shapes=list(scratch),
        cost_estimate=cost,
        compiler_params=pltpu.CompilerParams(vmem_limit_bytes=limit * 1024 * 1024),
    )(*arrays)


Z_GROUPS = [[y * Z + z for z in range(Z)] for y in range(Y)]
Y_GROUPS = [[y * Z + z for y in range(Y)] for z in range(Z)]


def exchange(value, groups, rows):
    peers = value.shape[0] // rows
    moved = lax.all_to_all(
        value.reshape(peers, rows, 1, DK), "tm", 0, 0, axis_index_groups=groups, tiled=True
    )
    return moved.reshape(value.shape)


def after(value, *others):
    return lax.optimization_barrier((value, *others))[0]


def body(queries, keys, values, log_decay, agent_ids, norm_gain, out_grad):
    ids = agent_ids.reshape(1, STEPS)
    gain = norm_gain.reshape(1, HEADS * DK)
    wide = (STEPS, HEADS * DK)
    plain, packed, totals = (Z * ROWS, DK), (Z * PACKED, DK), (Y * MESSAGE, DK)
    few = (Z, DK)
    long_cost = pl.CostEstimate(flops=40_000_000, bytes_accessed=2_000_000, transcendentals=65536)
    hbm = pl.BlockSpec(memory_space=pl.ANY)
    (ends,) = call(
        state_kernel, [(packed, F32)], keys, values, log_decay,
        specs=[hbm] * 3,
        outs=[hbm],
        scratch=[
            pltpu.VMEM(wide, BF16),
            pltpu.VMEM(wide, BF16),
            pltpu.VMEM((HEADS, STEPS), F32),
            pltpu.VMEM(packed, F32),
            pltpu.SemaphoreType.DMA((5,)),
        ],
        limit=60,
    )
    scores, weights, near, pull, scales, factor = call(
        local_kernel,
        [(wide, F32)] * 4 + [((STEPS, DK), F32), ((HEADS, DK), F32)],
        queries, keys, values, log_decay, ids, gain, out_grad,
        cost=long_cost,
    )
    ends = exchange(ends, Z_GROUPS, PACKED)
    local, factors, reach, row = call(
        row_scan_kernel, [(plain, F32), (few, F32), (few, F32), (totals, F32)], ends
    )
    rows = exchange(after(row, near), Y_GROUPS, MESSAGE)
    (entering,) = call(join_kernel, [(plain, F32)], rows, local, reach)
    state = exchange(entering, Z_GROUPS, ROWS)
    out, sums = call(
        output_kernel,
        [(wide, F32), ((8, 8, STEPS), F32)],
        queries, scales, pull, near, state,
    )
    sums = lax.all_to_all(sums, "head", 0, 0, tiled=True)
    adjoint, inverse, own = call(
        norm_kernel,
        [(wide, F32), ((STEPS, DK), F32), (packed, F32)],
        sums, out, queries, scales, pull, out_grad,
    )
    result, query_grad, near_dk, near_dv, near_dd = call(
        local_back_kernel,
        [(wide, BF16), (wide, BF16), (wide, F32), (wide, F32), ((HEADS, STEPS), F32)],
        queries, keys, values, scales, gain, scores, weights, out, inverse, state, adjoint,
        cost=long_cost,
    )
    own = exchange(own, Z_GROUPS, PACKED)
    local, row = call(row_scan_back_kernel, [(plain, F32), (totals, F32)], own, factors)
    row = exchange(row, Y_GROUPS, MESSAGE)
    (leaving,) = call(join_back_kernel, [(packed, F32)], row, local, factors, rows)
    end = exchange(leaving, Z_GROUPS, PACKED)
    key_grad, value_grad, decay_grad, gain_grad = call(
        final_kernel,
        [(wide, BF16), (wide, BF16), ((HEADS, STEPS), F32), ((1, HEADS * DK), F32)],
        keys, values, scales, factor, state, near_dk, near_dv, near_dd, end,
    )
    return result, query_grad, key_grad, value_grad, decay_grad, gain_grad.reshape(-1)


def solution(mesh):
    wide = P("tm", "head")
    return jax.shard_map(
        body,
        mesh=mesh,
        in_specs=(wide, wide, wide, P("head", "tm"), P("tm"), P("head"), wide),
        out_specs=(wide, wide, wide, wide, P("head", "tm"), P("head")),
        check_vma=False,
    )
```

```python
import jax
import jax.numpy as jnp
from jax import lax
from jax.experimental import pallas as pl
from jax.experimental.pallas import tpu as pltpu
from jax.sharding import PartitionSpec as P

DK = 128
STEPS = 128
HEADS = 4
TEAM = 16
WIDTH = 4096
EPS = 1e-06
CORES = 2
STAGGER_FIRST_NS = 5000
STAGGER_NS = 4000
SCALE = DK ** (-0.5)
Z = 16
Y = 4
OWNERS = Z // HEADS
ROWS = DK // OWNERS
PACKED = ROWS + 1
MESSAGE = ROWS + 2
TIMES = Y * Z
THIN = HEADS * DK // TIMES
THICK = THIN + 1
F32 = jnp.float32
BF16 = jnp.bfloat16

NN = (((1,), (0,)), ((), ()))
NT = (((1,), (1,)), ((), ()))
TN = (((0,), (0,)), ((), ()))


def mm(a, b, dims):
    return lax.dot_general(a, b, dims, preferred_element_type=F32)


def exact(a, b, dims):
    return lax.dot_general(
        a, b, dims, precision=lax.Precision.HIGHEST, preferred_element_type=F32
    )


def parts(a):
    high = a.astype(BF16)
    return high, (a - high.astype(F32)).astype(BF16)


def wide_left(a, b, dims):
    high, low = parts(a)
    return mm(high, b, dims) + mm(low, b, dims)


def wide_right(a, b, dims):
    high, low = parts(b)
    return mm(a, high, dims) + mm(a, low, dims)


def wide_both(a, b, dims):
    ah, al = parts(a)
    bh, bl = parts(b)
    return mm(ah, bh, dims) + (mm(ah, bl, dims) + mm(al, bh, dims))


def grid_index():
    rows = lax.broadcasted_iota(jnp.int32, (STEPS, STEPS), 0)
    cols = lax.broadcasted_iota(jnp.int32, (STEPS, STEPS), 1)
    return rows, cols


def head(ref, h):
    return ref[:, h * DK : (h + 1) * DK]


def slot(h, j):
    return (h * OWNERS + j) * PACKED


def spread_out(out_ref, h, state, row):
    for j in range(OWNERS):
        at = slot(h, j)
        out_ref[at : at + ROWS, :] = state[j * ROWS : (j + 1) * ROWS]
        out_ref[at + ROWS : at + PACKED, :] = row


def state_kernel(k_hbm, v_hbm, decay_hbm, out_hbm, k_ref, v_ref, decay_ref, out_ref, sems):
    loads = [
        pltpu.make_async_copy(source, target, sems.at[i])
        for i, (source, target) in enumerate(
            ((decay_hbm, decay_ref), (k_hbm, k_ref), (v_hbm, v_ref))
        )
    ]
    for load in loads:
        load.start()
    loads[0].wait()
    @pl.when(lax.axis_index("head") % CORES == 0)
    def _wait():
        pl.delay(STAGGER_FIRST_NS)

    rows, cols = grid_index()
    decay = decay_ref[...]
    tail = jnp.exp(exact((cols > rows).astype(F32), decay, NT))
    factor = jnp.exp(jnp.sum(decay, axis=1, keepdims=True))
    loads[1].wait()
    loads[2].wait()
    for h in range(HEADS):
        k = head(k_ref, h).astype(F32) * tail[:, h : h + 1]
        state = wide_left(k, head(v_ref, h), TN)
        row = jnp.broadcast_to(factor[h : h + 1], (1, DK))
        for j in range(DK // THIN):
            at = owner(h, j) * THICK
            out_ref[at : at + THIN, :] = state[j * THIN : (j + 1) * THIN]
            out_ref[at + THIN : at + THICK, :] = row
    store = pltpu.make_async_copy(out_ref, out_hbm, sems.at[3])
    store.start()
    store.wait()


def owner(h, j):
    return (j // OWNERS) * Z + h * OWNERS + j % OWNERS


def scan_kernel(in_ref, out_ref, own_ref, totals_ref, factor_ref):
    running = jnp.zeros((THIN, DK), F32)
    totals_ref[...] = jnp.zeros((2 * Y, DK), F32)
    for t in range(TIMES):
        at = t * THICK
        out_ref[t * THIN : (t + 1) * THIN, :] = running
        factor = in_ref[at + THIN : at + THICK, :]
        factor_ref[t : t + 1, :] = factor
        running = factor * running + in_ref[at : at + THIN, :]
        product = factor if t % Z == 0 else product * factor
        if t % Z == Z - 1:
            totals_ref[t // Z : t // Z + 1, :] = product
    mine = lax.axis_index("tm") // Z
    own_ref[...] = factor_ref[pl.ds(pl.multiple_of(mine * Z, Z), Z), :]


def state_of(ref, h):
    return jnp.concatenate(
        [ref[owner(h, j) * THIN : (owner(h, j) + 1) * THIN, :] for j in range(DK // THIN)], axis=0
    )


def row_scan_back_kernel(in_ref, factor_ref, local_ref, row_ref):
    running = jnp.zeros((ROWS, DK), F32)
    gain = jnp.zeros((1, DK), F32)
    for z in range(Z - 1, -1, -1):
        at = z * PACKED
        local_ref[z * ROWS : (z + 1) * ROWS, :] = running
        running = factor_ref[z : z + 1, :] * running + in_ref[at : at + ROWS, :]
        gain = gain + in_ref[at + ROWS : at + PACKED, :]
    for y in range(Y):
        row_ref[y * MESSAGE : y * MESSAGE + ROWS, :] = running
        row_ref[y * MESSAGE + ROWS : (y + 1) * MESSAGE, :] = jnp.broadcast_to(gain, (2, DK))


def join_back_kernel(rows_ref, local_ref, factor_ref, totals_ref, out_ref):
    mine = lax.axis_index("tm") // Z
    running = jnp.zeros((ROWS, DK), F32)
    for y in range(Y - 1, 0, -1):
        at = y * MESSAGE
        longer = totals_ref[y : y + 1, :] * running + rows_ref[at : at + ROWS, :]
        running = jnp.where(y > mine, longer, running)
    gain = rows_ref[ROWS:PACKED, :]
    for y in range(1, Y):
        gain = gain + rows_ref[y * MESSAGE + ROWS : y * MESSAGE + PACKED, :]
    product = jnp.ones((1, DK), F32)
    for z in range(Z - 1, -1, -1):
        at = z * PACKED
        out_ref[at : at + ROWS, :] = local_ref[z * ROWS : (z + 1) * ROWS, :] + product * running
        out_ref[at + ROWS : at + PACKED, :] = gain
        product = product * factor_ref[z : z + 1, :]


def decays(decay):
    rows, cols = grid_index()
    lower = (cols <= rows).astype(F32)
    column = exact(lower, decay, NT)
    row = exact(decay, lower, NT)
    return column, row


def weights_of(column, row, visible, h):
    spread = column[:, h : h + 1] - row[h : h + 1, :]
    return jnp.where(visible, jnp.exp(jnp.where(visible, spread, 0.0)), 0.0)


def visible_of(ids_ref):
    rows, cols = grid_index()
    team = jnp.broadcast_to((ids_ref[...] // TEAM).astype(F32), (STEPS, STEPS))
    return (cols <= rows) & (team == team.T)


def packed_state(ref, h):
    starts = [slot(h, j) for j in range(OWNERS)]
    return jnp.concatenate([ref[at : at + ROWS, :] for at in starts], axis=0)


def local_kernel(
    q_ref, k_ref, v_ref, decay_ref, ids_ref, gain_ref, grad_ref,
    scores_ref, weights_ref, out_ref, pull_ref, scales_ref, factor_ref,
):
    decay = decay_ref[...]
    column, row = decays(decay)
    rows, cols = grid_index()
    visible = visible_of(ids_ref)
    scales_ref[...] = jnp.zeros((STEPS, DK), F32)
    scales_ref[:, 0:HEADS] = jnp.exp(column) * SCALE
    scales_ref[:, HEADS : 2 * HEADS] = jnp.exp(exact((cols > rows).astype(F32), decay, NT))
    factor_ref[...] = jnp.broadcast_to(jnp.exp(jnp.sum(decay, axis=1, keepdims=True)), (HEADS, DK))
    for h in range(HEADS):
        span = slice(h * DK, (h + 1) * DK)
        weights = weights_of(column, row, visible, h) * SCALE
        scores = mm(head(q_ref, h), head(k_ref, h), NT) * weights
        weights_ref[:, span] = weights
        scores_ref[:, span] = scores
        out_ref[:, span] = wide_left(scores, head(v_ref, h), NN)
        pull_ref[:, span] = head(grad_ref, h).astype(F32) * head(gain_ref, h)


def grown_of(scales_ref, h):
    return scales_ref[:, h : h + 1]


def tail_of(scales_ref, h):
    return scales_ref[:, HEADS + h : HEADS + h + 1]


def output_kernel(q_ref, scales_ref, pull_ref, near_ref, state_ref, out_ref, sums_ref):
    squares = jnp.zeros((STEPS, DK), F32)
    inners = jnp.zeros((STEPS, DK), F32)
    for h in range(HEADS):
        span = slice(h * DK, (h + 1) * DK)
        inter = wide_right(head(q_ref, h), state_of(state_ref, h), NN)
        out = head(near_ref, h) + grown_of(scales_ref, h) * inter
        out_ref[:, span] = out
        squares = squares + out * out
        inners = inners + head(pull_ref, h) * out
    ones = jnp.ones((8, DK), F32)
    both = jnp.where(
        lax.broadcasted_iota(jnp.int32, (8, STEPS), 0) == 0,
        exact(ones, squares, NT),
        exact(ones, inners, NT),
    )
    for p in range(8):
        sums_ref[p] = both


def norm_kernel(sums_ref, o_ref, q_ref, scales_ref, pull_ref, grad_ref, adjoint_ref, inverse_ref, own_ref):
    @pl.when(lax.axis_index("head") % CORES == 0)
    def _wait():
        pl.delay(STAGGER_NS)

    total = sums_ref[0]
    for p in range(1, 8):
        total = total + sums_ref[p]
    inverse = 1.0 / jnp.sqrt(total[0:1] / WIDTH + EPS)
    back = total[1:2] * (inverse * inverse * inverse) / WIDTH
    both = jnp.concatenate([inverse, back, jnp.zeros((6, STEPS), F32)], axis=0).T
    inverse, back = both[:, 0:1], both[:, 1:2]
    inverse_ref[...] = jnp.broadcast_to(inverse, (STEPS, DK))
    for h in range(HEADS):
        out = head(o_ref, h)
        part = jnp.sum(head(grad_ref, h).astype(F32) * (out * inverse), axis=0, keepdims=True)
        adjoint = head(pull_ref, h) * inverse - out * back
        adjoint_ref[:, h * DK : (h + 1) * DK] = adjoint
        own = wide_right(head(q_ref, h), adjoint * grown_of(scales_ref, h), TN)
        spread_out(own_ref, h, own, part)


def local_back_kernel(
    q_ref, k_ref, v_ref, scales_ref, gain_ref, scores_ref, weights_ref, o_ref, inverse_ref, state_ref, adjoint_ref,
    result_ref, dq_ref, dk_ref, dv_ref, dd_ref,
):
    rows, cols = grid_index()
    until = (rows >= cols).astype(F32)
    inverse = inverse_ref[...]
    for h in range(HEADS):
        span = slice(h * DK, (h + 1) * DK)
        q, k, v = head(q_ref, h), head(k_ref, h), head(v_ref, h)
        result_ref[:, span] = (head(o_ref, h) * inverse * head(gain_ref, h)).astype(BF16)
        adjoint = head(adjoint_ref, h)
        scores = head(scores_ref, h)
        slopes = wide_left(adjoint, v, NT)
        joint = scores * slopes
        slopes = slopes * head(weights_ref, h)
        inter = wide_both(adjoint, state_of(state_ref, h), NT) * grown_of(scales_ref, h)
        dq_ref[:, span] = (wide_left(slopes, k, NN) + inter).astype(BF16)
        dk_ref[:, span] = wide_left(slopes, q, TN)
        dv_ref[:, span] = wide_both(scores, adjoint, TN)
        late = jnp.sum(joint + inter * q.astype(F32), axis=1, keepdims=True)
        columns = jnp.sum(joint, axis=0, keepdims=True)
        dd_ref[h : h + 1, :] = (
            jnp.sum(late * until, axis=0, keepdims=True)
            - exact(jnp.broadcast_to(columns, (8, STEPS)), until, NN)[0:1]
        )


def final_kernel(
    k_ref, v_ref, scales_ref, factor_ref, state_ref, near_dk_ref, near_dv_ref, near_dd_ref, end_ref,
    dk_ref, dv_ref, dd_ref, dg_ref,
):
    rows, cols = grid_index()
    before = (rows < cols).astype(F32)
    for h in range(HEADS):
        span = slice(h * DK, (h + 1) * DK)
        k, v = head(k_ref, h), head(v_ref, h)
        end = packed_state(end_ref, h)
        dk_end = wide_right(v, end, NT) * tail_of(scales_ref, h)
        dk_ref[:, span] = (head(near_dk_ref, h) + dk_end).astype(BF16)
        dv_end = wide_right(k, end, NN) * tail_of(scales_ref, h)
        dv_ref[:, span] = (head(near_dv_ref, h) + dv_end).astype(BF16)
        early = jnp.sum(dk_end * k.astype(F32), axis=1, keepdims=True)
        through = factor_ref[h : h + 1, :] * jnp.sum(end * state_of(state_ref, h))
        dd_ref[h : h + 1, :] = near_dd_ref[h : h + 1, :] + jnp.sum(early * before, axis=0, keepdims=True) + through
        dg_ref[:, span] = end_ref[slot(h, 0) + ROWS : slot(h, 0) + PACKED, :]


VMEM = pl.BlockSpec(memory_space=pltpu.VMEM)


def call(kernel, shapes, *arrays, specs=None, outs=None, scratch=(), cost=None, limit=16):
    return pl.pallas_call(
        kernel,
        out_shape=[jax.ShapeDtypeStruct(s, d) for s, d in shapes],
        in_specs=specs or [VMEM] * len(arrays),
        out_specs=outs or [VMEM] * len(shapes),
        scratch_shapes=list(scratch),
        cost_estimate=cost,
        compiler_params=pltpu.CompilerParams(vmem_limit_bytes=limit * 1024 * 1024),
    )(*arrays)


Z_GROUPS = [[y * Z + z for z in range(Z)] for y in range(Y)]
Y_GROUPS = [[y * Z + z for y in range(Y)] for z in range(Z)]


def exchange(value, groups, rows):
    peers = value.shape[0] // rows
    moved = lax.all_to_all(
        value.reshape(peers, rows, 1, DK), "tm", 0, 0, axis_index_groups=groups, tiled=True
    )
    return moved.reshape(value.shape)


def after(value, *others):
    return lax.optimization_barrier((value, *others))[0]


def body(queries, keys, values, log_decay, agent_ids, norm_gain, out_grad):
    ids = agent_ids.reshape(1, STEPS)
    gain = norm_gain.reshape(1, HEADS * DK)
    wide = (STEPS, HEADS * DK)
    plain, packed, totals = (Z * ROWS, DK), (Z * PACKED, DK), (Y * MESSAGE, DK)
    few = (Z, DK)
    thin, thick = (TIMES * THIN, DK), (TIMES * THICK, DK)
    long_cost = pl.CostEstimate(flops=40_000_000, bytes_accessed=2_000_000, transcendentals=65536)
    hbm = pl.BlockSpec(memory_space=pl.ANY)
    (ends,) = call(
        state_kernel, [(thick, F32)], keys, values, log_decay,
        specs=[hbm] * 3,
        outs=[hbm],
        scratch=[
            pltpu.VMEM(wide, BF16),
            pltpu.VMEM(wide, BF16),
            pltpu.VMEM((HEADS, STEPS), F32),
            pltpu.VMEM(thick, F32),
            pltpu.SemaphoreType.DMA((4,)),
        ],
        limit=60,
    )
    scores, weights, near, pull, scales, factor = call(
        local_kernel,
        [(wide, F32)] * 4 + [((STEPS, DK), F32), ((HEADS, DK), F32)],
        queries, keys, values, log_decay, ids, gain, out_grad,
        cost=long_cost,
    )
    ends = exchange(ends, None, THICK)
    entering, factors, rows = call(
        scan_kernel,
        [(thin, F32), (few, F32), ((2 * Y, DK), F32)],
        ends,
        scratch=[pltpu.VMEM((TIMES, DK), F32)],
    )
    state = exchange(after(entering, near), None, THIN)
    out, sums = call(
        output_kernel,
        [(wide, F32), ((8, 8, STEPS), F32)],
        queries, scales, pull, near, state,
    )
    sums = lax.all_to_all(sums, "head", 0, 0, tiled=True)
    adjoint, inverse, own = call(
        norm_kernel,
        [(wide, F32), ((STEPS, DK), F32), (packed, F32)],
        sums, out, queries, scales, pull, out_grad,
    )
    result, query_grad, near_dk, near_dv, near_dd = call(
        local_back_kernel,
        [(wide, BF16), (wide, BF16), (wide, F32), (wide, F32), ((HEADS, STEPS), F32)],
        queries, keys, values, scales, gain, scores, weights, out, inverse, state, adjoint,
        cost=long_cost,
    )
    own = exchange(own, Z_GROUPS, PACKED)
    local, row = call(row_scan_back_kernel, [(plain, F32), (totals, F32)], own, factors)
    row = exchange(row, Y_GROUPS, MESSAGE)
    (leaving,) = call(join_back_kernel, [(packed, F32)], row, local, factors, rows)
    end = exchange(leaving, Z_GROUPS, PACKED)
    key_grad, value_grad, decay_grad, gain_grad = call(
        final_kernel,
        [(wide, BF16), (wide, BF16), ((HEADS, STEPS), F32), ((1, HEADS * DK), F32)],
        keys, values, scales, factor, state, near_dk, near_dv, near_dd, end,
    )
    return result, query_grad, key_grad, value_grad, decay_grad, gain_grad.reshape(-1)


def solution(mesh):
    wide = P("tm", "head")
    return jax.shard_map(
        body,
        mesh=mesh,
        in_specs=(wide, wide, wide, P("head", "tm"), P("tm"), P("head"), wide),
        out_specs=(wide, wide, wide, wide, P("head", "tm"), P("head")),
        check_vma=False,
    )
```

```python
import jax
import jax.numpy as jnp
from jax import lax
from jax.experimental import pallas as pl
from jax.experimental.pallas import tpu as pltpu
from jax.sharding import PartitionSpec as P

DK = 128
STEPS = 128
HEADS = 4
TEAM = 16
WIDTH = 4096
EPS = 1e-06
CORES = 2
STAGGER_FIRST_NS = 4500
STAGGER_NS = 3500
SCALE = DK ** (-0.5)
Z = 16
Y = 4
OWNERS = Z // HEADS
ROWS = DK // OWNERS
PACKED = ROWS + 1
MESSAGE = ROWS + 2
TIMES = Y * Z
THIN = HEADS * DK // TIMES
THICK = THIN + 1
F32 = jnp.float32
BF16 = jnp.bfloat16

NN = (((1,), (0,)), ((), ()))
NT = (((1,), (1,)), ((), ()))
TN = (((0,), (0,)), ((), ()))


def mm(a, b, dims):
    return lax.dot_general(a, b, dims, preferred_element_type=F32)


def exact(a, b, dims):
    return lax.dot_general(
        a, b, dims, precision=lax.Precision.HIGHEST, preferred_element_type=F32
    )


def parts(a):
    high = a.astype(BF16)
    return high, (a - high.astype(F32)).astype(BF16)


def wide_left(a, b, dims):
    high, low = parts(a)
    return mm(high, b, dims) + mm(low, b, dims)


def wide_right(a, b, dims):
    high, low = parts(b)
    return mm(a, high, dims) + mm(a, low, dims)


def wide_both(a, b, dims):
    ah, al = parts(a)
    bh, bl = parts(b)
    return mm(ah, bh, dims) + (mm(ah, bl, dims) + mm(al, bh, dims))


def grid_index():
    rows = lax.broadcasted_iota(jnp.int32, (STEPS, STEPS), 0)
    cols = lax.broadcasted_iota(jnp.int32, (STEPS, STEPS), 1)
    return rows, cols


def head(ref, h):
    return ref[:, h * DK : (h + 1) * DK]


def slot(h, j):
    return (h * OWNERS + j) * PACKED


def spread_out(out_ref, h, state, row):
    for j in range(OWNERS):
        at = slot(h, j)
        out_ref[at : at + ROWS, :] = state[j * ROWS : (j + 1) * ROWS]
        out_ref[at + ROWS : at + PACKED, :] = row


def state_kernel(k_hbm, v_hbm, decay_hbm, out_hbm, k_ref, v_ref, decay_ref, out_ref, sems):
    loads = [
        pltpu.make_async_copy(source, target, sems.at[i])
        for i, (source, target) in enumerate(
            ((decay_hbm, decay_ref), (k_hbm, k_ref), (v_hbm, v_ref))
        )
    ]
    for load in loads:
        load.start()
    loads[0].wait()
    @pl.when(lax.axis_index("head") % CORES == 0)
    def _wait():
        pl.delay(STAGGER_FIRST_NS)

    rows, cols = grid_index()
    decay = decay_ref[...]
    tail = jnp.exp(exact((cols > rows).astype(F32), decay, NT))
    factor = jnp.exp(jnp.sum(decay, axis=1, keepdims=True))
    loads[1].wait()
    loads[2].wait()
    for h in range(HEADS):
        k = head(k_ref, h).astype(F32) * tail[:, h : h + 1]
        state = wide_left(k, head(v_ref, h), TN)
        row = jnp.broadcast_to(factor[h : h + 1], (1, DK))
        for j in range(DK // THIN):
            at = owner(h, j) * THICK
            out_ref[at : at + THIN, :] = state[j * THIN : (j + 1) * THIN]
            out_ref[at + THIN : at + THICK, :] = row
    store = pltpu.make_async_copy(out_ref, out_hbm, sems.at[3])
    store.start()
    store.wait()


def owner(h, j):
    return (j // OWNERS) * Z + h * OWNERS + j % OWNERS


def scan_kernel(in_ref, out_ref, own_ref, totals_ref, factor_ref):
    running = jnp.zeros((THIN, DK), F32)
    totals_ref[...] = jnp.zeros((2 * Y, DK), F32)
    for t in range(TIMES):
        at = t * THICK
        out_ref[t * THIN : (t + 1) * THIN, :] = running
        factor = in_ref[at + THIN : at + THICK, :]
        factor_ref[t : t + 1, :] = factor
        running = factor * running + in_ref[at : at + THIN, :]
        product = factor if t % Z == 0 else product * factor
        if t % Z == Z - 1:
            totals_ref[t // Z : t // Z + 1, :] = product
    mine = lax.axis_index("tm") // Z
    own_ref[...] = factor_ref[pl.ds(pl.multiple_of(mine * Z, Z), Z), :]


def state_of(ref, h):
    return jnp.concatenate(
        [ref[owner(h, j) * THIN : (owner(h, j) + 1) * THIN, :] for j in range(DK // THIN)], axis=0
    )


def row_scan_back_kernel(in_ref, factor_ref, local_ref, row_ref):
    running = jnp.zeros((ROWS, DK), F32)
    gain = jnp.zeros((1, DK), F32)
    for z in range(Z - 1, -1, -1):
        at = z * PACKED
        local_ref[z * ROWS : (z + 1) * ROWS, :] = running
        running = factor_ref[z : z + 1, :] * running + in_ref[at : at + ROWS, :]
        gain = gain + in_ref[at + ROWS : at + PACKED, :]
    for y in range(Y):
        row_ref[y * MESSAGE : y * MESSAGE + ROWS, :] = running
        row_ref[y * MESSAGE + ROWS : (y + 1) * MESSAGE, :] = jnp.broadcast_to(gain, (2, DK))


def join_back_kernel(rows_ref, local_ref, factor_ref, totals_ref, out_ref):
    mine = lax.axis_index("tm") // Z
    running = jnp.zeros((ROWS, DK), F32)
    for y in range(Y - 1, 0, -1):
        at = y * MESSAGE
        longer = totals_ref[y : y + 1, :] * running + rows_ref[at : at + ROWS, :]
        running = jnp.where(y > mine, longer, running)
    gain = rows_ref[ROWS:PACKED, :]
    for y in range(1, Y):
        gain = gain + rows_ref[y * MESSAGE + ROWS : y * MESSAGE + PACKED, :]
    product = jnp.ones((1, DK), F32)
    for z in range(Z - 1, -1, -1):
        at = z * PACKED
        out_ref[at : at + ROWS, :] = local_ref[z * ROWS : (z + 1) * ROWS, :] + product * running
        out_ref[at + ROWS : at + PACKED, :] = gain
        product = product * factor_ref[z : z + 1, :]


def decays(decay):
    rows, cols = grid_index()
    lower = (cols <= rows).astype(F32)
    column = exact(lower, decay, NT)
    row = exact(decay, lower, NT)
    return column, row


def weights_of(column, row, visible, h):
    spread = column[:, h : h + 1] - row[h : h + 1, :]
    return jnp.where(visible, jnp.exp(jnp.where(visible, spread, 0.0)), 0.0)


def visible_of(ids_ref):
    rows, cols = grid_index()
    team = jnp.broadcast_to((ids_ref[...] // TEAM).astype(F32), (STEPS, STEPS))
    return (cols <= rows) & (team == team.T)


def packed_state(ref, h):
    starts = [slot(h, j) for j in range(OWNERS)]
    return jnp.concatenate([ref[at : at + ROWS, :] for at in starts], axis=0)


def local_kernel(
    q_ref, k_ref, v_ref, decay_ref, ids_ref, gain_ref, grad_ref,
    scores_ref, weights_ref, out_ref, pull_ref, scales_ref, factor_ref,
):
    decay = decay_ref[...]
    column, row = decays(decay)
    rows, cols = grid_index()
    visible = visible_of(ids_ref)
    scales_ref[...] = jnp.zeros((STEPS, DK), F32)
    scales_ref[:, 0:HEADS] = jnp.exp(column) * SCALE
    scales_ref[:, HEADS : 2 * HEADS] = jnp.exp(exact((cols > rows).astype(F32), decay, NT))
    factor_ref[...] = jnp.broadcast_to(jnp.exp(jnp.sum(decay, axis=1, keepdims=True)), (HEADS, DK))
    for h in range(HEADS):
        span = slice(h * DK, (h + 1) * DK)
        weights = weights_of(column, row, visible, h) * SCALE
        scores = mm(head(q_ref, h), head(k_ref, h), NT) * weights
        weights_ref[:, span] = weights
        scores_ref[:, span] = scores
        out_ref[:, span] = wide_left(scores, head(v_ref, h), NN)
        pull_ref[:, span] = head(grad_ref, h).astype(F32) * head(gain_ref, h)


def grown_of(scales_ref, h):
    return scales_ref[:, h : h + 1]


def tail_of(scales_ref, h):
    return scales_ref[:, HEADS + h : HEADS + h + 1]


def output_kernel(q_ref, scales_ref, pull_ref, near_ref, state_ref, out_ref, sums_ref):
    squares = jnp.zeros((STEPS, DK), F32)
    inners = jnp.zeros((STEPS, DK), F32)
    for h in range(HEADS):
        span = slice(h * DK, (h + 1) * DK)
        inter = wide_right(head(q_ref, h), state_of(state_ref, h), NN)
        out = head(near_ref, h) + grown_of(scales_ref, h) * inter
        out_ref[:, span] = out
        squares = squares + out * out
        inners = inners + head(pull_ref, h) * out
    ones = jnp.ones((8, DK), F32)
    both = jnp.where(
        lax.broadcasted_iota(jnp.int32, (8, STEPS), 0) == 0,
        exact(ones, squares, NT),
        exact(ones, inners, NT),
    )
    for p in range(8):
        sums_ref[p] = both


def norm_kernel(sums_ref, o_ref, q_ref, scales_ref, pull_ref, grad_ref, adjoint_ref, inverse_ref, own_ref):
    @pl.when(lax.axis_index("head") % CORES == 0)
    def _wait():
        pl.delay(STAGGER_NS)

    total = sums_ref[0]
    for p in range(1, 8):
        total = total + sums_ref[p]
    inverse = 1.0 / jnp.sqrt(total[0:1] / WIDTH + EPS)
    back = total[1:2] * (inverse * inverse * inverse) / WIDTH
    both = jnp.concatenate([inverse, back, jnp.zeros((6, STEPS), F32)], axis=0).T
    inverse, back = both[:, 0:1], both[:, 1:2]
    inverse_ref[...] = jnp.broadcast_to(inverse, (STEPS, DK))
    for h in range(HEADS):
        out = head(o_ref, h)
        part = jnp.sum(head(grad_ref, h).astype(F32) * (out * inverse), axis=0, keepdims=True)
        adjoint = head(pull_ref, h) * inverse - out * back
        adjoint_ref[:, h * DK : (h + 1) * DK] = adjoint
        own = wide_right(head(q_ref, h), adjoint * grown_of(scales_ref, h), TN)
        spread_out(own_ref, h, own, part)


def local_back_kernel(
    q_ref, k_ref, v_ref, scales_ref, gain_ref, scores_ref, weights_ref, o_ref, inverse_ref, state_ref, adjoint_ref,
    result_ref, dq_ref, dk_ref, dv_ref, dd_ref,
):
    rows, cols = grid_index()
    until = (rows >= cols).astype(F32)
    inverse = inverse_ref[...]
    for h in range(HEADS):
        span = slice(h * DK, (h + 1) * DK)
        q, k, v = head(q_ref, h), head(k_ref, h), head(v_ref, h)
        result_ref[:, span] = (head(o_ref, h) * inverse * head(gain_ref, h)).astype(BF16)
        adjoint = head(adjoint_ref, h)
        scores = head(scores_ref, h)
        slopes = wide_left(adjoint, v, NT)
        joint = scores * slopes
        slopes = slopes * head(weights_ref, h)
        inter = wide_both(adjoint, state_of(state_ref, h), NT) * grown_of(scales_ref, h)
        dq_ref[:, span] = (wide_left(slopes, k, NN) + inter).astype(BF16)
        dk_ref[:, span] = wide_left(slopes, q, TN)
        dv_ref[:, span] = wide_both(scores, adjoint, TN)
        late = jnp.sum(joint + inter * q.astype(F32), axis=1, keepdims=True)
        columns = jnp.sum(joint, axis=0, keepdims=True)
        dd_ref[h : h + 1, :] = (
            jnp.sum(late * until, axis=0, keepdims=True)
            - exact(jnp.broadcast_to(columns, (8, STEPS)), until, NN)[0:1]
        )


def final_kernel(
    k_ref, v_ref, scales_ref, factor_ref, state_ref, near_dk_ref, near_dv_ref, near_dd_ref, end_ref,
    dk_ref, dv_ref, dd_ref, dg_ref,
):
    rows, cols = grid_index()
    before = (rows < cols).astype(F32)
    for h in range(HEADS):
        span = slice(h * DK, (h + 1) * DK)
        k, v = head(k_ref, h), head(v_ref, h)
        end = packed_state(end_ref, h)
        dk_end = wide_right(v, end, NT) * tail_of(scales_ref, h)
        dk_ref[:, span] = (head(near_dk_ref, h) + dk_end).astype(BF16)
        dv_end = wide_right(k, end, NN) * tail_of(scales_ref, h)
        dv_ref[:, span] = (head(near_dv_ref, h) + dv_end).astype(BF16)
        early = jnp.sum(dk_end * k.astype(F32), axis=1, keepdims=True)
        through = factor_ref[h : h + 1, :] * jnp.sum(end * state_of(state_ref, h))
        dd_ref[h : h + 1, :] = near_dd_ref[h : h + 1, :] + jnp.sum(early * before, axis=0, keepdims=True) + through
        dg_ref[:, span] = end_ref[slot(h, 0) + ROWS : slot(h, 0) + PACKED, :]


VMEM = pl.BlockSpec(memory_space=pltpu.VMEM)


def call(kernel, shapes, *arrays, specs=None, outs=None, scratch=(), cost=None, limit=16):
    return pl.pallas_call(
        kernel,
        out_shape=[jax.ShapeDtypeStruct(s, d) for s, d in shapes],
        in_specs=specs or [VMEM] * len(arrays),
        out_specs=outs or [VMEM] * len(shapes),
        scratch_shapes=list(scratch),
        cost_estimate=cost,
        compiler_params=pltpu.CompilerParams(vmem_limit_bytes=limit * 1024 * 1024),
    )(*arrays)


Z_GROUPS = [[y * Z + z for z in range(Z)] for y in range(Y)]
Y_GROUPS = [[y * Z + z for y in range(Y)] for z in range(Z)]


def exchange(value, groups, rows):
    peers = value.shape[0] // rows
    moved = lax.all_to_all(
        value.reshape(peers, rows, 1, DK), "tm", 0, 0, axis_index_groups=groups, tiled=True
    )
    return moved.reshape(value.shape)


def after(value, *others):
    return lax.optimization_barrier((value, *others))[0]


def body(queries, keys, values, log_decay, agent_ids, norm_gain, out_grad):
    ids = agent_ids.reshape(1, STEPS)
    gain = norm_gain.reshape(1, HEADS * DK)
    wide = (STEPS, HEADS * DK)
    plain, packed, totals = (Z * ROWS, DK), (Z * PACKED, DK), (Y * MESSAGE, DK)
    few = (Z, DK)
    thin, thick = (TIMES * THIN, DK), (TIMES * THICK, DK)
    long_cost = pl.CostEstimate(flops=40_000_000, bytes_accessed=2_000_000, transcendentals=65536)
    hbm = pl.BlockSpec(memory_space=pl.ANY)
    (ends,) = call(
        state_kernel, [(thick, F32)], keys, values, log_decay,
        specs=[hbm] * 3,
        outs=[hbm],
        scratch=[
            pltpu.VMEM(wide, BF16),
            pltpu.VMEM(wide, BF16),
            pltpu.VMEM((HEADS, STEPS), F32),
            pltpu.VMEM(thick, F32),
            pltpu.SemaphoreType.DMA((4,)),
        ],
        limit=60,
    )
    scores, weights, near, pull, scales, factor = call(
        local_kernel,
        [(wide, F32)] * 4 + [((STEPS, DK), F32), ((HEADS, DK), F32)],
        queries, keys, values, log_decay, ids, gain, out_grad,
        cost=long_cost,
    )
    ends = exchange(ends, None, THICK)
    entering, factors, rows = call(
        scan_kernel,
        [(thin, F32), (few, F32), ((2 * Y, DK), F32)],
        ends,
        scratch=[pltpu.VMEM((TIMES, DK), F32)],
    )
    state = exchange(after(entering, near), None, THIN)
    out, sums = call(
        output_kernel,
        [(wide, F32), ((8, 8, STEPS), F32)],
        queries, scales, pull, near, state,
    )
    sums = lax.all_to_all(sums, "head", 0, 0, tiled=True)
    adjoint, inverse, own = call(
        norm_kernel,
        [(wide, F32), ((STEPS, DK), F32), (packed, F32)],
        sums, out, queries, scales, pull, out_grad,
    )
    result, query_grad, near_dk, near_dv, near_dd = call(
        local_back_kernel,
        [(wide, BF16), (wide, BF16), (wide, F32), (wide, F32), ((HEADS, STEPS), F32)],
        queries, keys, values, scales, gain, scores, weights, out, inverse, state, adjoint,
        cost=long_cost,
    )
    own = exchange(own, Z_GROUPS, PACKED)
    local, row = call(row_scan_back_kernel, [(plain, F32), (totals, F32)], own, factors)
    row = exchange(row, Y_GROUPS, MESSAGE)
    (leaving,) = call(join_back_kernel, [(packed, F32)], row, local, factors, rows)
    end = exchange(leaving, Z_GROUPS, PACKED)
    key_grad, value_grad, decay_grad, gain_grad = call(
        final_kernel,
        [(wide, BF16), (wide, BF16), ((HEADS, STEPS), F32), ((1, HEADS * DK), F32)],
        keys, values, scales, factor, state, near_dk, near_dv, near_dd, end,
    )
    return result, query_grad, key_grad, value_grad, decay_grad, gain_grad.reshape(-1)


def solution(mesh):
    wide = P("tm", "head")
    return jax.shard_map(
        body,
        mesh=mesh,
        in_specs=(wide, wide, wide, P("head", "tm"), P("tm"), P("head"), wide),
        out_specs=(wide, wide, wide, wide, P("head", "tm"), P("head")),
        check_vma=False,
    )
```
